32 devices in a mesh: dp: 4 (over y, core), row: 2 (over x), col: 4 (over z).
Axes of the slice: x: 2, y: 2, z: 4, core: 2. Of those that a mesh axis runs over, the one named last changes fastest.
Arguments:
- inputs: bfloat16 [2048, 6144], P('dp', 'row'), may hold values from -600 to 600
- saved_qkv: bfloat16 [2048, 3, 3072], P('dp', None, 'col'), may hold values from -6 to 6
- saved_up: bfloat16 [2048, 12288], P('dp', 'col'), may hold values from -6 to 6
- cotangent: bfloat16 [2048, 6144], P('dp', 'row'), may hold values from -6 to 6
- weight_qkv: bfloat16 [6144, 3, 3072], P('row', None, 'col'), may hold values from -0.078125 to 0.078125
- weight_up: bfloat16 [6144, 12288], P('row', 'col'), may hold values from -0.078125 to 0.078125
- weight_attn: bfloat16 [3072, 6144], P('col', 'row'), may hold values from -0.109375 to 0.109375
- weight_down: bfloat16 [12288, 6144], P('col', 'row'), may hold values from -0.0546875 to 0.0546875
Outputs:
- grad_inputs: bfloat16 [2048, 6144], P(('dp', 'col'), 'row')
- grad_qkv: bfloat16 [2, 4, 768, 3, 3072], P('row', 'dp', None, None, 'col')
- grad_up: bfloat16 [2, 4, 768, 12288], P('row', 'dp', None, 'col')
- grad_attn: bfloat16 [4, 4, 192, 6144], P('col', 'dp', None, 'row')
- grad_down: bfloat16 [4, 4, 768, 6144], P('col', 'dp', None, 'row')
The draws below stay inside these ranges and needn't reach their ends.
All inputs are finite; a program needn't handle non-finite values.
Results may differ from the reference program's by a relative error of at most 0.0039.
The reference program's roundings to bfloat16 on the way count: a program that leaves them out, or rounds other values in their place, can miss the bound.
Values may be sent and summed in bfloat16 or wider, within the bound.
No kernel may reach another device: no remote copies, remote signals or barrier semaphores. Data moves between devices by JAX's collectives and lax.ppermute only.
A program may use at most 192 MiB of HBM per device.

```python
import math
import jax
import jax.numpy as jnp
from jax import lax

D = 6144
H = 24
HD = 128
FF = 12288
S = 256
A = 3072
IMAGES = 8
TOKENS = 2048
D_SUB = 768
A_SUB = 192
F_SUB = 768
N_DP = 4
N_ROW = 2
N_COL = 4


def draw_inputs(key, part):
    keys = jax.random.split(jax.random.fold_in(key, 11), 4)
    columns = jnp.arange(D, dtype=jnp.float32) / D
    spread = jnp.exp(jax.random.uniform(keys[1], (D,), jnp.float32, 0.0, math.log(10.0)))
    base = jax.random.truncated_normal(keys[0], -4.0, 4.0, (TOKENS, D), jnp.float32)
    ramp = jnp.exp(columns * (0.5 * math.log(3.0)))
    rowscale = jnp.exp(jax.random.uniform(keys[3], (TOKENS, 1), jnp.float32, 0.0, math.log(4.0)))
    values = base * spread * ramp * rowscale * 0.25
    return values.astype(jnp.bfloat16)


def steps_of(own_key, dims, pieces, low, largest):
    def one(dim, blocks):
        draws = jax.random.uniform(jax.random.fold_in(jax.random.fold_in(own_key, 6), dim), (blocks,), jnp.float32, low / len(pieces), largest / len(pieces))
        return jnp.repeat(jnp.exp(draws), dims[dim] // blocks).reshape((-1,) + (1,) * (len(dims) - dim - 1))

    loudness = one(*pieces[0])
    for cut in pieces[1:]:
        loudness = loudness * one(*cut)
    return loudness


def bell_draw(stream_key, dims, scale, most, pieces=(), kind=jnp.bfloat16):
    array = scale * jax.random.normal(stream_key, dims, jnp.float32)
    if pieces:
        array = array * steps_of(stream_key, dims, pieces, -0.22, 0.18)
    return jnp.clip(array, -most, most).astype(kind)


def setup_inputs(seed: int = 0) -> dict:
    seeds = jax.random.split(jax.random.key(seed), 9)
    inputs = draw_inputs(jax.random.fold_in(seeds[8], 71), 0)
    saved_qkv = bell_draw(seeds[1], (TOKENS, 3, A), 1.0, 6.0, ((0, 4), (2, 4)))
    saved_up = bell_draw(seeds[2], (TOKENS, FF), 1.0, 6.0, ((0, 4), (1, 4)))
    cotangent = bell_draw(seeds[3], (TOKENS, D), 1.0, 6.0, ((0, 4), (1, 2)))
    weight_qkv = bell_draw(seeds[4], (D, 3, A), D ** -0.5, 0.078125, ((0, 2), (2, 4)))
    weight_up = bell_draw(seeds[5], (D, FF), D ** -0.5, 0.078125, ((0, 2), (1, 4)))
    weight_attn = bell_draw(seeds[6], (A, D), A ** -0.5, 0.109375, ((0, 4), (1, 2)))
    weight_down = bell_draw(seeds[7], (FF, D), FF ** -0.5, 0.0546875, ((0, 4), (1, 2)))
    return dict(inputs=inputs, saved_qkv=saved_qkv, saved_up=saved_up, cotangent=cotangent, weight_qkv=weight_qkv, weight_up=weight_up, weight_attn=weight_attn, weight_down=weight_down)


EPS = 1e-06
SQRT_HALF = 0.7071067811865476
INV_ROOT_TWO_PI = 0.3989422804014327

def gelu_exact(values):
    return 0.5 * values * (1.0 + jax.scipy.special.erf(values * SQRT_HALF))

def gelu_slope(values):
    cumul = 0.5 * (1.0 + jax.scipy.special.erf(values * SQRT_HALF))
    return cumul + values * jnp.exp(-0.5 * values * values) * INV_ROOT_TWO_PI

def head_norm(values):
    average = lax.optimization_barrier(jnp.mean(values, axis=-1, keepdims=True))
    centred = values - average
    inv_std = lax.rsqrt(lax.optimization_barrier(jnp.mean(centred * centred, axis=-1, keepdims=True)) + EPS)
    return (centred * inv_std, inv_std)

def head_norm_back(normed, inv_std, upstream):
    first = lax.optimization_barrier(jnp.mean(upstream, axis=-1, keepdims=True))
    cross = lax.optimization_barrier(jnp.mean(upstream * normed, axis=-1, keepdims=True))
    return inv_std * (upstream - first - normed * cross)

def reference(inputs, saved_qkv, saved_up, cotangent, weight_qkv, weight_up, weight_attn, weight_down):
    f32 = jnp.float32
    bf16 = jnp.bfloat16
    values = inputs.astype(f32)
    average = lax.optimization_barrier(jnp.sum(values, axis=1, keepdims=True)) / D
    second = lax.optimization_barrier(jnp.sum(values * values, axis=1, keepdims=True)) / D
    inv_std = lax.rsqrt(second - average * average + EPS)
    normed = (values - average) * inv_std
    normed_b = normed.astype(bf16)
    qkv5 = saved_qkv.reshape(IMAGES, S, 3, H, HD)
    query = qkv5[:, :, 0]
    keyed = qkv5[:, :, 1]
    valued = qkv5[:, :, 2]
    q_norm, q_inv = head_norm(query.astype(f32))
    k_norm, k_inv = head_norm(keyed.astype(f32))
    qn_b = q_norm.astype(bf16)
    kn_b = k_norm.astype(bf16)
    scale = HD ** (-0.5)
    scores = jnp.einsum('bqhd,bkhd->bhqk', qn_b.astype(f32), kn_b.astype(f32)) * scale
    expo = jnp.exp(scores)
    probs = expo / lax.optimization_barrier(jnp.sum(expo, axis=-1, keepdims=True))
    probs_b = probs.astype(bf16)
    attended = jnp.einsum('bhqk,bkhd->bqhd', probs_b.astype(f32), valued.astype(f32)).astype(bf16)
    attended = attended.reshape(TOKENS, A)
    up_vals = saved_up.astype(f32)
    hidden_b = gelu_exact(up_vals).astype(bf16)
    grad_o = jnp.dot(cotangent, weight_attn.T, preferred_element_type=f32).astype(bf16)
    grad_hidden = jnp.dot(cotangent, weight_down.T, preferred_element_type=f32)
    grad_pre = (grad_hidden * gelu_slope(up_vals)).astype(bf16)
    grad_o4 = grad_o.reshape(IMAGES, S, H, HD)
    grad_probs = jnp.einsum('bqhd,bkhd->bhqk', grad_o4.astype(f32), valued.astype(f32))
    grad_value = jnp.einsum('bhqk,bqhd->bkhd', probs_b.astype(f32), grad_o4.astype(f32)).astype(bf16)
    rowdot = lax.optimization_barrier(jnp.sum(probs * grad_probs, axis=-1, keepdims=True))
    grad_scores = (probs * (grad_probs - rowdot) * scale).astype(bf16)
    grad_qn = jnp.einsum('bhqk,bkhd->bqhd', grad_scores.astype(f32), kn_b.astype(f32))
    grad_kn = jnp.einsum('bhqk,bqhd->bkhd', grad_scores.astype(f32), qn_b.astype(f32))
    grad_query = head_norm_back(q_norm, q_inv, grad_qn).astype(bf16)
    grad_key = head_norm_back(k_norm, k_inv, grad_kn).astype(bf16)
    grad_flat = jnp.stack([grad_query, grad_key, grad_value], axis=2).reshape(TOKENS, 3 * A)
    flat_weight = weight_qkv.reshape(D, 3 * A)
    grad_normed = jnp.dot(grad_flat, flat_weight.T, preferred_element_type=f32)
    grad_normed = grad_normed + jnp.dot(grad_pre, weight_up.T, preferred_element_type=f32)
    mean_grad = lax.optimization_barrier(jnp.sum(grad_normed, axis=1, keepdims=True)) / D
    mean_cross = lax.optimization_barrier(jnp.sum(grad_normed * normed, axis=1, keepdims=True)) / D
    grad_inputs = (cotangent.astype(f32) + inv_std * (grad_normed - mean_grad - normed * mean_cross)).astype(bf16)
    full_qkv = jnp.dot(normed_b.T, grad_flat, preferred_element_type=f32).astype(bf16)
    grad_qkv = full_qkv.reshape(N_ROW, N_DP, D_SUB, 3, A)
    full_up = jnp.dot(normed_b.T, grad_pre, preferred_element_type=f32).astype(bf16)
    grad_up = full_up.reshape(N_ROW, N_DP, D_SUB, FF)
    full_attn = jnp.dot(attended.T, cotangent, preferred_element_type=f32).astype(bf16)
    grad_attn = full_attn.reshape(N_COL, N_DP, A_SUB, D)
    full_down = jnp.dot(hidden_b.T, cotangent, preferred_element_type=f32).astype(bf16)
    grad_down = full_down.reshape(N_COL, N_DP, F_SUB, D)
    return (grad_inputs, grad_qkv, grad_up, grad_attn, grad_down)
```

```python
import math

import jax
import jax.numpy as jnp
from jax import lax
from jax.experimental import pallas as pl
from jax.experimental.pallas import tpu as pltpu
from jax.sharding import PartitionSpec as P

HD = 128
S = 256

EPS = 1e-06
SQRT_HALF = 0.7071067811865476
INV_ROOT_TWO_PI = 0.3989422804014327

F32 = jnp.float32
BF16 = jnp.bfloat16
VMEM_LIMIT = 60 * 1024 * 1024


def swap(value, axis, bit):
    size = lax.axis_size(axis)
    return lax.ppermute(value, axis, [(i, i ^ bit) for i in range(size)])


def dot_nt(a, b):
    return lax.dot_general(a, b, (((1,), (1,)), ((), ())), preferred_element_type=F32)


def dot_tn(a, b):
    return lax.dot_general(a, b, (((0,), (0,)), ((), ())), preferred_element_type=F32)


def tile_of(size, most):
    best = size
    if size > most:
        best = 128
        for t in range(128, most + 1, 128):
            if size % t == 0:
                best = t
    return best


def params(**kw):
    return pltpu.CompilerParams(vmem_limit_bytes=VMEM_LIMIT, **kw)


def cost(flops, moved, trans=0):
    return pl.CostEstimate(flops=int(flops), bytes_accessed=int(moved), transcendentals=int(trans))


def head_norm(values):
    average = jnp.mean(values, axis=-1, keepdims=True)
    centred = values - average
    inv_std = lax.rsqrt(jnp.mean(centred * centred, axis=-1, keepdims=True) + EPS)
    return centred * inv_std, inv_std


def head_norm_back(normed, inv_std, upstream):
    first = jnp.mean(upstream, axis=-1, keepdims=True)
    cross = jnp.mean(upstream * normed, axis=-1, keepdims=True)
    return inv_std * (upstream - first - normed * cross)


def attn_partial(cot, weight):
    rows, depth = cot.shape
    width = weight.shape[0]
    tile = tile_of(width, 384)

    def kernel(c_ref, w_ref, loc_ref):
        loc_ref[...] = dot_nt(c_ref[...], w_ref[...])

    return pl.pallas_call(
        kernel,
        grid=(width // tile,),
        in_specs=[
            pl.BlockSpec((rows, depth), lambda i: (0, 0)),
            pl.BlockSpec((tile, depth), lambda i: (i, 0)),
        ],
        out_specs=pl.BlockSpec((rows, tile), lambda i: (0, i)),
        out_shape=jax.ShapeDtypeStruct((rows, width), F32),
        compiler_params=params(),
        cost_estimate=cost(2 * rows * depth * width, 2 * (rows + width) * depth + 4 * rows * width),
        name="attn_partial",
    )(cot, weight)


def down_partial(where, cot, weight, up, n_dp, n_col):
    rows, depth = cot.shape
    ups = up.shape[1]
    sub = ups // n_dp
    half = rows // 2
    quad = half // n_col

    def kernel(s_ref, c_ref, w_ref, u_ref, la_ref, lb_ref, sa_ref, sb_ref, own, near, far):
        r = pl.program_id(0)
        u = u_ref[...].astype(F32)
        cumul = 0.5 * (1.0 + lax.erf(u * SQRT_HALF))
        slope = cumul + u * jnp.exp(-0.5 * u * u) * INV_ROOT_TWO_PI
        hidden = (u * cumul).astype(BF16)
        acc = (dot_nt(c_ref[...], w_ref[...]) * slope).reshape(n_col, 2, quad, sub)
        low = acc[:, 0].reshape(half, sub)
        high = acc[:, 1].reshape(half, sub)
        la_ref[...] = low
        sa_ref[...] = low.astype(BF16)
        lb_ref[...] = high
        sb_ref[...] = high.astype(BF16)

        @pl.when(r == 0)
        def _():
            own[...] = hidden

        @pl.when(r == 1)
        def _():
            near[...] = hidden

        @pl.when(r >= 2)
        def _():
            h = s_ref[1]
            far[h] = hidden[:half]
            far[1 - h] = hidden[half:]

    def col(r, s):
        return jnp.bitwise_xor(s[0], r)

    chunk = pl.BlockSpec((half, sub), lambda r, s: (0, col(r, s)))
    return pl.pallas_call(
        kernel,
        grid_spec=pltpu.PrefetchScalarGridSpec(
            num_scalar_prefetch=1,
            grid=(n_dp,),
            in_specs=[
                pl.BlockSpec((rows, depth), lambda r, s: (0, 0)),
                pl.BlockSpec((sub, depth), lambda r, s: (col(r, s), 0)),
                pl.BlockSpec((rows, sub), lambda r, s: (0, col(r, s))),
            ],
            out_specs=[
                chunk,
                chunk,
                chunk,
                chunk,
                pl.BlockSpec((rows, sub), lambda r, s: (0, 0)),
                pl.BlockSpec((rows, sub), lambda r, s: (0, 0)),
                pl.BlockSpec((None, 2, half, sub), lambda r, s: (jnp.maximum(r - 2, 0), 0, 0, 0)),
            ],
        ),
        out_shape=[
            jax.ShapeDtypeStruct((half, ups), F32),
            jax.ShapeDtypeStruct((half, ups), F32),
            jax.ShapeDtypeStruct((half, ups), BF16),
            jax.ShapeDtypeStruct((half, ups), BF16),
            jax.ShapeDtypeStruct((rows, sub), BF16),
            jax.ShapeDtypeStruct((rows, sub), BF16),
            jax.ShapeDtypeStruct((2, 2, half, sub), BF16),
        ],
        compiler_params=params(),
        cost_estimate=cost(
            2 * rows * depth * ups, 2 * (rows + ups) * depth + 10 * rows * ups, 2 * rows * ups
        ),
        name="down_partial",
    )(where, cot, weight, up)


def norm_split(where, inputs, average, inv_std, n_dp):
    rows, width = inputs.shape
    sub = width // n_dp
    half = rows // 2
    if sub % 128:
        normed = ((inputs.astype(F32) - average) * inv_std).astype(BF16)

        def piece(r):
            at = jnp.bitwise_xor(where[0], r) * sub
            return lax.dynamic_slice_in_dim(normed, at, sub, 1)

        both = jnp.stack([piece(2), piece(3)])
        return piece(0), piece(1), lax.dynamic_slice_in_dim(both, where[1] * half, half, 1)

    def kernel(s_ref, x_ref, a_ref, i_ref, own_ref, near_ref, far_ref):
        r = pl.program_id(0)

        @pl.when(r < 2)
        def _():
            out = ((x_ref[...].astype(F32) - a_ref[...]) * i_ref[...]).astype(BF16)

            @pl.when(r == 0)
            def _():
                own_ref[...] = out

            @pl.when(r == 1)
            def _():
                near_ref[...] = out

        @pl.when(r >= 2)
        def _():
            at = pl.ds(pl.multiple_of(s_ref[1] * half, half), half)
            far_ref[...] = ((x_ref[at, :].astype(F32) - a_ref[at, :]) * i_ref[at, :]).astype(BF16)

    return pl.pallas_call(
        kernel,
        grid_spec=pltpu.PrefetchScalarGridSpec(
            num_scalar_prefetch=1,
            grid=(4,),
            in_specs=[
                pl.BlockSpec((rows, sub), lambda r, s: (0, jnp.bitwise_xor(s[0], r))),
                pl.BlockSpec((rows, 1), lambda r, s: (0, 0)),
                pl.BlockSpec((rows, 1), lambda r, s: (0, 0)),
            ],
            out_specs=[
                pl.BlockSpec((rows, sub), lambda r, s: (0, 0)),
                pl.BlockSpec((rows, sub), lambda r, s: (0, 0)),
                pl.BlockSpec((None, half, sub), lambda r, s: (jnp.maximum(r - 2, 0), 0, 0)),
            ],
        ),
        out_shape=[
            jax.ShapeDtypeStruct((rows, sub), BF16),
            jax.ShapeDtypeStruct((rows, sub), BF16),
            jax.ShapeDtypeStruct((2, half, sub), BF16),
        ],
        compiler_params=params(),
        cost_estimate=cost(8 * rows * width, 4 * rows * width),
        name="norm_split",
    )(where, inputs, average, inv_std)


def attention(where, qkv, o_local, o_recv, n_dp):
    _, rows, cols = qkv.shape
    images = rows // S
    heads = cols // HD
    sub = cols // n_dp
    scale = HD ** (-0.5)

    def kernel(s_ref, x_ref, loc_ref, rec_ref, flat_ref, close_ref, far_ref):
        b = pl.program_id(0)
        me = s_ref[0]
        h = s_ref[1]
        grad_o = (loc_ref[...] + rec_ref[...]).astype(BF16)
        outs = []
        for n in range(heads):
            at = slice(n * HD, (n + 1) * HD)
            q_norm, q_inv = head_norm(x_ref[0, :, at].astype(F32))
            k_norm, k_inv = head_norm(x_ref[1, :, at].astype(F32))
            qn_b = q_norm.astype(BF16)
            kn_b = k_norm.astype(BF16)
            v = x_ref[2, :, at]
            go = grad_o[:, at]
            expo = jnp.exp(dot_nt(qn_b, kn_b) * scale)
            probs = expo * pl.reciprocal(jnp.sum(expo, axis=-1, keepdims=True), approx=False)
            probs_b = probs.astype(BF16)
            outs.append(jnp.dot(probs_b, v, preferred_element_type=F32).astype(BF16))
            grad_probs = dot_nt(go, v)
            flat_ref[2, :, at] = dot_tn(probs_b, go).astype(BF16)
            rowdot = jnp.sum(probs * grad_probs, axis=-1, keepdims=True)
            grad_s = (probs * (grad_probs - rowdot) * scale).astype(BF16)
            grad_qn = jnp.dot(grad_s, kn_b, preferred_element_type=F32)
            grad_kn = dot_tn(grad_s, qn_b)
            flat_ref[0, :, at] = head_norm_back(q_norm, q_inv, grad_qn).astype(BF16)
            flat_ref[1, :, at] = head_norm_back(k_norm, k_inv, grad_kn).astype(BF16)
        whole = jnp.concatenate(outs, axis=1)
        for j in range(n_dp):
            slot = jnp.bitwise_xor(me, j)
            piece = whole[:, j * sub : (j + 1) * sub]

            @pl.when(slot < 2)
            def _(slot=slot, piece=piece):
                close_ref[slot] = piece

            @pl.when(slot >= 2)
            def _(slot=slot, piece=piece):
                far_ref[slot - 2, jnp.bitwise_xor(b, h)] = piece

    return pl.pallas_call(
        kernel,
        grid_spec=pltpu.PrefetchScalarGridSpec(
            num_scalar_prefetch=1,
            grid=(images,),
            in_specs=[
                pl.BlockSpec((3, S, cols), lambda b, s: (0, b, 0)),
                pl.BlockSpec((S, cols), lambda b, s: (b, 0)),
                pl.BlockSpec((S, cols), lambda b, s: (b, 0)),
            ],
            out_specs=[
                pl.BlockSpec((3, S, cols), lambda b, s: (0, b, 0)),
                pl.BlockSpec((2, S, sub), lambda b, s: (0, b, 0)),
                pl.BlockSpec((2, images, S, sub), lambda b, s: (0, 0, 0, 0)),
            ],
        ),
        out_shape=[
            jax.ShapeDtypeStruct((3, rows, cols), BF16),
            jax.ShapeDtypeStruct((2, rows, sub), BF16),
            jax.ShapeDtypeStruct((2, images, S, sub), BF16),
        ],
        compiler_params=params(),
        cost_estimate=cost(12 * rows * S * cols, 20 * rows * cols, rows * S * heads),
        name="attention",
    )(where, qkv, o_local, o_recv)


def normed_grad(where, flat_part, pre, w_up, n_col, chunk):
    half, ups = pre.shape
    width = w_up.shape[0]
    share = half // n_col
    tile = tile_of(width, 512)
    parts = flat_part.reshape(n_col, 2, share, width)

    def kernel(s_ref, f_ref, p_ref, wu_ref, own_ref, *rest):
        sends, acc_ref = rest[:-1], rest[-1]
        acc_ref[...] = dot_nt(p_ref[...], wu_ref[...]).reshape(n_col, share, tile) + f_ref[...]
        z = s_ref[2]
        own_ref[...] = acc_ref[z]
        for r in range(1, n_col):
            sends[r - 1][...] = acc_ref[jnp.bitwise_xor(z, r)].astype(BF16)

    out = pl.BlockSpec((share, tile), lambda i, s: (0, i))
    return pl.pallas_call(
        kernel,
        grid_spec=pltpu.PrefetchScalarGridSpec(
            num_scalar_prefetch=1,
            grid=(width // tile,),
            in_specs=[
                pl.BlockSpec((n_col, None, share, tile), lambda i, s: (0, chunk, 0, i)),
                pl.BlockSpec((half, ups), lambda i, s: (0, 0)),
                pl.BlockSpec((tile, ups), lambda i, s: (i, 0)),
            ],
            out_specs=[out] * n_col,
            scratch_shapes=[pltpu.VMEM((n_col, share, tile), F32)],
        ),
        out_shape=[jax.ShapeDtypeStruct((share, width), F32)]
        + [jax.ShapeDtypeStruct((share, width), BF16)] * (n_col - 1),
        compiler_params=params(),
        cost_estimate=cost(
            2 * half * width * ups, 2 * (half + width) * ups + 6 * half * width
        ),
        name="normed_grad",
    )(where, parts, pre, w_up)


def weight_grad(lhs_sets, rhs_parts, outs, grid, rhs_bytes, name):
    ops = []

    def place(group):
        at = []
        for part in group:
            at.append(list(range(len(ops), len(ops) + len(part))))
            ops.extend(part)
        return at

    lhs_at = [place(group) for group in lhs_sets]
    rhs_at = place(rhs_parts)

    def kernel(*refs):
        def read(part):
            vals = []
            for i in part:
                v = refs[i][...]
                vals.append(v.reshape(-1, v.shape[-1]))
            return vals[0] if len(vals) == 1 else jnp.concatenate(vals, axis=0)

        right = [read(part) for part in rhs_at]
        for s, group in enumerate(lhs_at):
            acc = None
            for part, r in zip(group, right):
                term = dot_tn(read(part), r)
                acc = term if acc is None else acc + term
            refs[len(ops) + s][...] = acc.astype(BF16)

    total = sum(math.prod(shape.shape) for shape, _ in outs)
    depth = rhs_bytes[0]
    return pl.pallas_call(
        kernel,
        grid=grid,
        in_specs=[spec for _, spec in ops],
        out_specs=[spec for _, spec in outs],
        out_shape=[shape for shape, _ in outs],
        compiler_params=params(),
        cost_estimate=cost(2 * total * depth, 2 * total + 2 * depth * rhs_bytes[1]),
        name=name,
    )(*[a for a, _ in ops])


def fixed(shape, index=None):
    where = index if index is not None else (0,) * len(shape)
    return pl.BlockSpec(shape, lambda *_: where)


def body(inputs, saved_qkv, saved_up, cotangent, weight_qkv, weight_up, weight_attn, weight_down):
    tok_rows, feat_local = inputs.shape
    head_cols = saved_qkv.shape[2]
    up_cols = saved_up.shape[1]
    n_dp = lax.axis_size("dp")
    n_row = lax.axis_size("row")
    n_col = lax.axis_size("col")
    assert n_dp == 4 and n_row % 2 == 0 and n_col % 2 == 0
    width = feat_local * n_row
    half = tok_rows // 2
    sub = feat_local // n_dp
    f_sub = up_cols // n_dp
    a_sub = head_cols // n_dp
    share = tok_rows // n_col

    me = lax.axis_index("dp")
    my_row = lax.axis_index("row")
    my_col = lax.axis_index("col")
    h = jnp.bitwise_and(jnp.bitwise_xor(my_row, my_col), 1)
    where = jnp.stack([me, h, my_col]).astype(jnp.int32)

    def near(v):
        return swap(v, "dp", 1)

    def far(v):
        return swap(v, "dp", 2)

    def row_sum(local):
        if n_row == 2:
            return local + swap(local, "row", 1)
        return lax.psum(local, "row")

    def row_pair(local, send):
        if n_row == 2:
            return local, swap(send, "row", 1)
        return lax.psum(local, "row"), jnp.zeros_like(send)

    def after(value, *others):
        return lax.optimization_barrier((value,) + others)[0]

    cot_mine = lax.dynamic_slice_in_dim(cotangent, h * half, half, 0)
    cot_f2m = far(cot_mine)

    o_local = attn_partial(after(cotangent, cot_mine), weight_attn)
    o_local, o_recv = row_pair(o_local, o_local)

    values = after(inputs, o_local).astype(F32)
    sums = row_sum(jnp.stack([jnp.sum(values, axis=1), jnp.sum(values * values, axis=1)]))
    average = (sums[0] / width)[:, None]
    inv_std = lax.rsqrt((sums[1] / width)[:, None] - average * average + EPS)
    cot_near = near(cotangent)

    lo_local, hi_local, lo_send, hi_send, hid_own, hid_next, hid_far = down_partial(
        after(where, o_local), cotangent, weight_down, saved_up, n_dp, n_col
    )
    lo_local, lo_recv = row_pair(lo_local, lo_send)
    hi_local, hi_recv = row_pair(hi_local, hi_send)
    hid_f2 = far(hid_far)
    hid_near = near(hid_next)

    nrm_own, nrm_next, nrm_far = norm_split(after(where, lo_send), inputs, average, inv_std, n_dp)
    nrm_f2m = far(nrm_far)
    nrm_near = near(nrm_next)

    cot_f2o = swap(cot_f2m, "col", 1)
    cot_f3m = near(cot_f2m)

    qkv3 = jnp.transpose(saved_qkv, (1, 0, 2))
    flat, att_close, att_far = attention(after(where, nrm_own), qkv3, o_local, o_recv, n_dp)
    att_f2 = far(att_far)
    att_near = near(att_close[1])
    flat_mine = lax.dynamic_slice_in_dim(flat, h * half, half, 1)
    flat_f2m = far(flat_mine)
    flat_near = near(flat)

    wq3 = jnp.transpose(weight_qkv, (1, 0, 2))
    flat_part = jnp.einsum("xta,xda->td", flat, wq3, preferred_element_type=F32)

    lo_pre = (after(lo_local, flat_part) + lo_recv.astype(F32)).astype(BF16)
    lo_mine = lax.dynamic_slice_in_dim(lo_pre, h * (half // 2), half // 2, 0)
    lo_f2m = far(lo_mine)
    lo_near = near(lo_pre)
    lo_parts = normed_grad(where, flat_part, lo_pre, weight_up, n_col, 0)
    lo_got = [swap(lo_parts[r], "col", r) for r in range(1, n_col)]

    cot_f3o = near(cot_f2o)
    hid_f3 = near(hid_f2[1])
    att_f3 = near(att_f2[1])

    tile = tile_of(feat_local, 512)

    def wide(rows_):
        return pl.BlockSpec((rows_, tile), lambda i: (0, i))

    grad_down, grad_attn = weight_grad(
        [
            [
                [(hid_own, fixed((tok_rows, f_sub)))],
                [(hid_near, fixed((tok_rows, f_sub)))],
                [(hid_f2, fixed((None, 2, half, f_sub)))],
                [(hid_f3, fixed((2, half, f_sub)))],
            ],
            [
                [(att_close, fixed((None, tok_rows, a_sub)))],
                [(att_near, fixed((tok_rows, a_sub)))],
                [(att_f2, fixed((None, 2, half, a_sub)))],
                [(att_f3, fixed((2, half, a_sub)))],
            ],
        ],
        [
            [(after(cotangent, lo_parts[0]), wide(tok_rows))],
            [(cot_near, wide(tok_rows))],
            [(cot_f2m, wide(half)), (cot_f2o, wide(half))],
            [(cot_f3m, wide(half)), (cot_f3o, wide(half))],
        ],
        [
            (jax.ShapeDtypeStruct((f_sub, feat_local), BF16), wide(f_sub)),
            (jax.ShapeDtypeStruct((a_sub, feat_local), BF16), wide(a_sub)),
        ],
        (feat_local // tile,),
        (4 * tok_rows, feat_local),
        "grad_down_attn",
    )

    hi_pre = (after(hi_local, grad_attn) + hi_recv.astype(F32)).astype(BF16)
    hi_mine = lax.dynamic_slice_in_dim(hi_pre, h * (half // 2), half // 2, 0)
    hi_f2m = far(hi_mine)
    hi_near = near(hi_pre)
    hi_parts = normed_grad(where, flat_part, hi_pre, weight_up, n_col, 1)
    hi_got = [swap(hi_parts[r], "col", r) for r in range(1, n_col)]

    nrm_f2o = swap(nrm_f2m, "col", 1)
    nrm_f3m = near(nrm_f2m[1])
    nrm_f3o = near(nrm_f2o[1])
    flat_f2o = swap(flat_f2m, "row", 1)
    flat_f3m = near(flat_f2m)
    flat_f3o = near(flat_f2o)

    def trio(rows_):
        return pl.BlockSpec((None, rows_, head_cols), lambda i: (i, 0, 0))

    (grad_qkv,) = weight_grad(
        [
            [
                [(after(nrm_own, hi_parts[0]), fixed((tok_rows, sub)))],
                [(nrm_near, fixed((tok_rows, sub)))],
                [(nrm_f2m, fixed((None, half, sub))), (nrm_f2o, fixed((None, half, sub)))],
                [(nrm_f3m, fixed((half, sub))), (nrm_f3o, fixed((half, sub)))],
            ]
        ],
        [
            [(flat, trio(tok_rows))],
            [(flat_near, trio(tok_rows))],
            [(flat_f2m, trio(half)), (flat_f2o, trio(half))],
            [(flat_f3m, trio(half)), (flat_f3o, trio(half))],
        ],
        [(jax.ShapeDtypeStruct((3, sub, head_cols), BF16), trio(sub))],
        (3,),
        (4 * tok_rows, 3 * head_cols),
        "grad_qkv",
    )

    lo_f2o = swap(lo_f2m, "row", 1)
    lo_f3m = near(lo_f2m)
    lo_f3o = near(lo_f2o)
    hi_f2o = swap(hi_f2m, "row", 1)
    hi_f3m = near(hi_f2m)
    hi_f3o = near(hi_f2o)

    quad = half // n_col
    tile_u = tile_of(up_cols, 512)

    def cut(v, count):
        lead = v.shape[:-2]
        seen = v.reshape(lead + (count, 2, quad, sub))
        none = (None,) * len(lead)
        zero = (0,) * len(lead)
        return [
            (seen, fixed(none + (count, None, quad, sub), zero + (0, c, 0, 0))) for c in range(2)
        ]

    def wide_u(rows_):
        return pl.BlockSpec((rows_, tile_u), lambda i: (0, i))

    few = n_col // 2
    (grad_up,) = weight_grad(
        [
            [
                cut(nrm_own, n_col),
                cut(nrm_near, n_col),
                cut(nrm_f2m, few) + cut(nrm_f2o, few),
                cut(nrm_f3m, few) + cut(nrm_f3o, few),
            ]
        ],
        [
            [(after(lo_pre, grad_qkv), wide_u(half)), (hi_pre, wide_u(half))],
            [(lo_near, wide_u(half)), (hi_near, wide_u(half))],
            [(v, wide_u(half // 2)) for v in (lo_f2m, hi_f2m, lo_f2o, hi_f2o)],
            [(v, wide_u(half // 2)) for v in (lo_f3m, hi_f3m, lo_f3o, hi_f3o)],
        ],
        [(jax.ShapeDtypeStruct((sub, up_cols), BF16), wide_u(sub))],
        (up_cols // tile_u,),
        (4 * tok_rows, up_cols),
        "grad_up",
    )

    def gathered(parts, got):
        acc = parts[0]
        for g in got:
            acc = acc + g.astype(F32)
        return acc

    grad_normed = jnp.concatenate([gathered(lo_parts, lo_got), gathered(hi_parts, hi_got)])
    first = my_col * share
    x_share = lax.dynamic_slice_in_dim(inputs, first, share, 0).astype(F32)
    avg_share = lax.dynamic_slice_in_dim(average, first, share, 0)
    inv_share = lax.dynamic_slice_in_dim(inv_std, first, share, 0)
    cot_share = lax.dynamic_slice_in_dim(cotangent, first, share, 0)
    normed_share = (x_share - avg_share) * inv_share
    back = row_sum(
        jnp.stack([jnp.sum(grad_normed, axis=1), jnp.sum(grad_normed * normed_share, axis=1)])
    )
    branch = (
        grad_normed - (back[0] / width)[:, None] - normed_share * (back[1] / width)[:, None]
    )
    grad_inputs = (cot_share.astype(F32) + inv_share * branch).astype(BF16)

    grad_qkv = jnp.transpose(grad_qkv, (1, 0, 2)).reshape(1, 1, sub, 3, head_cols)
    return (
        grad_inputs,
        grad_qkv,
        grad_up.reshape(1, 1, sub, up_cols),
        grad_attn.reshape(1, 1, a_sub, feat_local),
        grad_down.reshape(1, 1, f_sub, feat_local),
    )


def solution(mesh):
    return jax.shard_map(
        body,
        mesh=mesh,
        in_specs=(
            P("dp", "row"),
            P("dp", None, "col"),
            P("dp", "col"),
            P("dp", "row"),
            P("row", None, "col"),
            P("row", "col"),
            P("col", "row"),
            P("col", "row"),
        ),
        out_specs=(
            P(("dp", "col"), "row"),
            P("row", "dp", None, None, "col"),
            P("row", "dp", None, "col"),
            P("col", "dp", None, "row"),
            P("col", "dp", None, "row"),
        ),
        check_vma=False,
    )
```
